32 devices in a mesh: gx: 4 (over z), gy: 8 (over y, x, core).
Axes of the slice: x: 2, y: 2, z: 4, core: 2. Of those that a mesh axis runs over, the one named last changes fastest.
Arguments:
- sensitivity: float32 [3, 262144], P(None, ('gx', 'gy')), may hold values from -24 to 24
- node_weight: float32 [262144], P(('gx', 'gy')), may hold values from 0.05 to 0.5
- dest_device: int32 [262144, 1], P(('gx', 'gy')), may hold values from 0 to 31; in each aligned block of 8192 rows (0 to 8191, 8192 to 16383, ...) at most 512 rows name the same one
- dest_cell: int32 [262144], P(('gx', 'gy')), may hold values from 0 to 131071
- box_owner: int32 [262144, 1], P(('gx', 'gy')), may hold values from 0 to 31; in each aligned block of 8192 rows (0 to 8191, 8192 to 16383, ...) at most 512 rows name the same one
- box_slot: int32 [262144], P(('gx', 'gy')), may hold values from 0 to 63
- stiffness: float32 [64, 256, 256], P('gx', 'gy'), may hold values from 0.5 to 2
- anchor: float32 [3, 64, 256, 256], P(None, 'gx', 'gy'), may hold values from 3 to 6
- coupling: float32 [9, 64, 256, 256], P(None, 'gx', 'gy'), may hold values from -1 to 1
Outputs:
- adjoint: float32 [3, 64, 256, 256], P(None, 'gx', 'gy')
- box_gradient: float32 [3, 2048], P(None, ('gx', 'gy'))
The draws below stay inside these ranges and needn't reach their ends.
Inputs may be any that keep to these rules, and one draw needn't show every extreme that they name: `dest_device`: among the rows of one device, no deformation device is named more than 512 times, and in some device's rows one is named exactly 512 times. `box_owner`: among the rows of one device, no owner is named more than 512 times, and in some device's rows one is named exactly 512 times.
All inputs are finite; a program needn't handle non-finite values.
Results may differ from the reference program's by a relative error of at most 0.0003.
Values sent between devices are 32-bit elements; how exact they have to be, the bound alone decides.
A program may use at most 192 MiB of HBM per device.

```python
import math
import jax
import jax.numpy as jnp
import numpy as np

CX = 16
CY = 32
CZ = 256
SR_DEV = 8192
BOX_DEV = 64
SWEEPS = 4
CAP = 512
NX = 64
NY = 256
NZ = 256
ROWS = 262144
BOXES = 2048
N_GX = 4
N_GY = 8


def set_ends(result, own_key, smallest, high):
    place = [jax.random.randint(jax.random.fold_in(own_key, axis), (), 0, length) for axis, length in enumerate(result.shape)]
    longest = result.shape.index(max(result.shape))
    neighbour = place[:longest] + [(place[longest] + 1) % result.shape[longest]] + place[longest + 1:]
    return result.at[tuple(place)].set(smallest).at[tuple(neighbour)].set(high)


def levels(rng, shape, cuts, least, high):
    def one(position, parts):
        heights = jax.random.uniform(jax.random.fold_in(jax.random.fold_in(rng, 6), position), (parts,), jnp.float32, least / len(cuts), high / len(cuts))
        return jnp.repeat(jnp.exp(heights), shape[position] // parts).reshape((-1,) + (1,) * (len(shape) - position - 1))

    gain = one(*cuts[0])
    for cut in cuts[1:]:
        gain = gain * one(*cut)
    return gain


def assign_block(own_key, own, number, rows, number_of, top, most, lean):
    sequence = jax.random.permutation(own_key, number_of)
    heavy_load, common = load_shares(number_of, rows * top, most, lean, True), load_shares(number_of, rows * top, most, lean, False)
    places = jnp.arange(number_of)

    def named(tallies, rotation):
        used = int((tallies > 0).sum())
        fixed = max(1, used // 4)
        moved = fixed + (places - fixed + rotation * (used - fixed)) % max(1, number_of - fixed)
        return jnp.zeros((number_of,), jnp.int32).at[sequence[jnp.where(places < fixed, places, moved)]].set(jnp.asarray(tallies, jnp.int32))

    tallies = jnp.where(number % 4 == 0, named(heavy_load, number // 4), named(common, number - number // 4 - 1))
    mixed = jax.random.permutation(jax.random.fold_in(own, 3), number_of)
    donor, receiver = mixed[0:number_of // 2 * 2:2], mixed[1:number_of // 2 * 2:2]
    slack = jnp.minimum(tallies[donor] - 1, most - tallies[receiver]) // 2
    slack = jnp.where((donor == sequence[0]) | (receiver == sequence[0]) | (tallies[receiver] == 0), 0, jnp.maximum(slack, 0))
    moved = jax.random.randint(jax.random.fold_in(own, 4), (number_of // 2,), 0, 1 << 20) % (slack + 1)
    tallies = tallies.at[donor].add(-moved).at[receiver].add(moved)
    labels = jnp.searchsorted(jnp.cumsum(tallies), jnp.arange(rows * top), side="right").astype(jnp.int32)
    grid = labels.reshape(top, rows).T
    grid = grid[jax.random.permutation(jax.random.fold_in(own, 1), rows)]
    rotation = jax.random.randint(jax.random.fold_in(own, 2), (rows, 1), 0, top)
    return jnp.take_along_axis(grid, (jnp.arange(top)[None, :] + rotation) % top, axis=1)


def load_shares(count, total, limit, lean, full):
    loads = [(1 << 20) // math.isqrt(grade ** lean) + 1 for grade in range(1, count + 1)]
    largest = limit if full else min(limit, max(-(-total // count), total * loads[0] // sum(loads)))
    least = 1 if total - largest >= count - 1 else 0
    counts, surplus = [largest] + [least] * (count - 1), total - largest - least * (count - 1)
    while surplus > 0:
        candidates = [i for i in range(1, count) if counts[i] < largest] or [i for i in range(1, count) if counts[i] < limit]
        mass, left = sum([loads[i] for i in candidates]), surplus
        for i in candidates:
            extra = min(limit - counts[i], max(1, left * loads[i] // mass), surplus)
            counts[i] = counts[i] + extra
            surplus = surplus - extra
    return np.array(counts)


def noise(rng, shape, width, bound, split=(), dtype=jnp.bfloat16):
    array = jax.random.normal(rng, shape, jnp.float32) * width
    if len(split) > 0:
        array = levels(rng, shape, split, -0.22, 0.18) * array
    return jnp.clip(array, min=-bound, max=bound).astype(dtype)


def setup_inputs(seed: int = 0) -> dict:
    keys = jax.random.split(jax.random.key(seed), 10)
    sensitivity = noise(keys[0], (3, ROWS), 4.0, 24.0, ((1, 32),), jnp.float32)
    node_weight = jnp.clip(0.05 + 0.45 * jax.random.uniform(keys[1], (ROWS,), jnp.float32) ** levels(keys[1], (ROWS,), ((0, 32),), -0.2, 0.2), 0.05, 0.5)
    dest_device_keys = jax.random.split(jax.random.fold_in(keys[2], 1), ROWS // SR_DEV)
    dest_device_turns = jax.random.permutation(jax.random.fold_in(keys[2], 3), ROWS // SR_DEV)
    dest_device = jax.vmap(lambda own, number: assign_block(jax.random.fold_in(keys[2], 2), own, number, SR_DEV, N_GX * N_GY, 1, CAP, 2))(dest_device_keys, dest_device_turns).reshape((ROWS, 1))
    dest_cell = set_ends(jax.random.randint(keys[3], (ROWS,), 0, CX * CY * CZ), jax.random.fold_in(keys[3], 1), 0, (CX * CY * CZ) - 1).astype(jnp.int32)
    box_owner_keys = jax.random.split(jax.random.fold_in(keys[4], 1), ROWS // SR_DEV)
    box_owner_turns = jax.random.permutation(jax.random.fold_in(keys[4], 3), ROWS // SR_DEV)
    box_owner = jax.vmap(lambda own, number: assign_block(jax.random.fold_in(keys[4], 2), own, number, SR_DEV, N_GX * N_GY, 1, CAP, 1))(box_owner_keys, box_owner_turns).reshape((ROWS, 1))
    box_slot = set_ends(jax.random.randint(keys[5], (ROWS,), 0, BOX_DEV), jax.random.fold_in(keys[5], 1), 0, BOX_DEV - 1).astype(jnp.int32)
    stiffness = jnp.clip(jnp.exp(math.log(2.0) - 1.3862944 * jax.random.uniform(keys[6], (NX, NY, NZ), jnp.float32) ** levels(keys[6], (NX, NY, NZ), ((0, 4), (1, 8)), -0.2, 0.2)), 0.5, 2.0)
    anchor = jnp.clip(jnp.exp(math.log(6.0) - 0.6931472 * jax.random.uniform(keys[7], (3, NX, NY, NZ), jnp.float32) ** levels(keys[7], (3, NX, NY, NZ), ((1, 4), (2, 8)), -0.2, 0.2)), 3.0, 6.0)
    coupling = jnp.clip(jax.random.uniform(keys[8], (9, NX, NY, NZ), jnp.float32, -1.0, 1.0) * levels(keys[8], (9, NX, NY, NZ), ((1, 4), (2, 8)), -0.4, 0.0), -1.0, 1.0)
    return dict(sensitivity=sensitivity, node_weight=node_weight, dest_device=dest_device, dest_cell=dest_cell, box_owner=box_owner, box_slot=box_slot, stiffness=stiffness, anchor=anchor, coupling=coupling)


def neighbour_sum(padded):
    z_padded = jnp.pad(padded, ((0, 0), (0, 0), (0, 0), (1, 1)))
    middle = z_padded[:, 1:-1, 1:-1, :]
    total = z_padded[:, 2:, 1:-1, 1:-1] + z_padded[:, :-2, 1:-1, 1:-1]
    total = total + z_padded[:, 1:-1, 2:, 1:-1] + z_padded[:, 1:-1, :-2, 1:-1]
    return total + middle[..., 2:] + middle[..., :-2]


def apply_transposed(field, weighted_pad, stiff, anchor, coupling):
    blocks = coupling.reshape((3, 3) + coupling.shape[1:])
    mixing = jnp.sum(blocks * field[:, None], axis=0)
    return 6.0 * stiff[None] * field - neighbour_sum(weighted_pad) + mixing + anchor * field


def reference(sensitivity, node_weight, dest_device, dest_cell, box_owner, box_slot, stiffness, anchor, coupling):
    target = dest_device[:, 0]
    local_cell = dest_cell
    x_cell = (target // N_GY) * CX + local_cell // (CY * CZ)
    y_cell = (target % N_GY) * CY + (local_cell // CZ) % CY
    z_cell = local_cell % CZ
    flat_ids = ((x_cell * NY + y_cell) * NZ + z_cell).astype(jnp.int32)
    load = jnp.zeros((3, NX * NY * NZ), jnp.float32).at[:, flat_ids].add(sensitivity)
    load = load.reshape(3, NX, NY, NZ)
    diagonal = 6.0 * stiffness[None] + anchor + jnp.stack([coupling[0], coupling[4], coupling[8]])
    adjoint = jnp.zeros((3, NX, NY, NZ), jnp.float32)
    for sweep_idx in range(SWEEPS):
        weighted = jnp.pad(stiffness[None] * adjoint, ((0, 0), (1, 1), (1, 1), (0, 0)))
        applied = apply_transposed(adjoint, weighted, stiffness, anchor, coupling)
        adjoint = adjoint + (load - applied) / diagonal
    flat_field = adjoint.reshape(3, NX * NY * NZ)
    row_gradient = node_weight[None] * flat_field[:, flat_ids]
    box_ids = (box_owner[:, 0] * BOX_DEV + box_slot).astype(jnp.int32)
    box_gradient = jax.ops.segment_sum(row_gradient.T, box_ids, num_segments=BOXES).T
    return adjoint, box_gradient
```

```python
import functools

import jax
import jax.numpy as jnp
from jax import lax
from jax.experimental import pallas as pl
from jax.experimental.pallas import tpu as pltpu
from jax.sharding import PartitionSpec as P

BOX_DEV = 64
SWEEPS = 4
NT = (((1,), (1,)), ((), ()))
F32 = jnp.float32
BF16 = jnp.bfloat16
MESH = pl.DeviceIdType.MESH


def two_terms(x):
    hi = x.astype(BF16).astype(F32)
    return hi, x - hi


def matches(count, row):
    return lax.broadcasted_iota(jnp.int32, (count, row.shape[1]), 0) == row


def one_hot(mask):
    return jnp.where(mask, 1.0, 0.0).astype(BF16)


def scaled(mask, row):
    return jnp.where(mask, row, 0.0).astype(BF16)


def dot_nt(a, b):
    return lax.dot_general(a, b, NT, preferred_element_type=F32)


def pack_kernel(size_z, step, sens, weight, device, cell, owner, slot, out, tri, seen):
    targets, fields, capacity = out.shape
    rows = sens.shape[1]
    out[...] = jnp.zeros_like(out)
    seen[...] = jnp.zeros_like(seen)
    tri[...] = one_hot(
        lax.broadcasted_iota(jnp.int32, (step, step), 0)
        < lax.broadcasted_iota(jnp.int32, (step, step), 1)
    )

    def block(index, carry):
        span = pl.ds(pl.multiple_of(index * step, step), step)
        target = device[:, span]
        chosen = matches(targets, target)
        before = jnp.dot(one_hot(chosen), tri[...], preferred_element_type=F32) + seen[:, :1]
        rank = jnp.sum(jnp.where(chosen, before, 0.0), axis=0, keepdims=True).astype(jnp.int32)
        seen[...] = seen[...] + jnp.sum(jnp.where(chosen, 1.0, 0.0), axis=1, keepdims=True)
        place = one_hot(matches(capacity, rank))
        cells = cell[:, span]
        payload = jnp.concatenate(
            [
                sens[:, span],
                weight[:, span],
                (cells % size_z).astype(F32),
                (cells // size_z).astype(F32),
                owner[:, span].astype(F32),
                slot[:, span].astype(F32),
            ],
            axis=0,
        )
        wide = (targets, fields, step)
        to = lax.broadcasted_iota(jnp.int32, wide, 0) == target[None]
        total = jnp.zeros((targets * fields, capacity), F32)
        for term in two_terms(payload):
            lhs = jnp.where(to, term[None], 0.0).reshape(targets * fields, step).astype(BF16)
            total = total + dot_nt(lhs, place)
        out[...] = out[...] + total.reshape(targets, fields, capacity)
        return carry

    lax.fori_loop(0, rows // step, block, 0)


def pack_rows(size_z, devices, capacity, sens, weight, device, cell, owner, slot):
    step = min(512, sens.shape[1])
    return pl.pallas_call(
        functools.partial(pack_kernel, size_z, step),
        out_shape=jax.ShapeDtypeStruct((devices, 8, capacity), F32),
        in_specs=[pl.BlockSpec(memory_space=pltpu.VMEM)] * 6,
        out_specs=pl.BlockSpec(memory_space=pltpu.VMEM),
        scratch_shapes=[pltpu.VMEM((step, step), BF16), pltpu.VMEM((devices, 128), F32)],
        name="pack_rows",
    )(sens, weight, device, cell, owner, slot)


def joined(ref):
    return jnp.concatenate([ref[i] for i in range(ref.shape[0])], axis=1)


def scatter_kernel(arrived, load):
    parts, size_xy, size_z = load.shape

    @pl.when(pl.program_id(0) == 0)
    def _():
        load[...] = jnp.zeros_like(load)

    block = joined(arrived)
    at_z = matches(size_z, block[4:5].astype(jnp.int32))
    at_xy = one_hot(matches(size_xy, block[5:6].astype(jnp.int32)))
    for k in range(parts):
        hi, lo = two_terms(block[k : k + 1])
        load[k] = load[k] + dot_nt(at_xy, scaled(at_z, hi)) + dot_nt(at_xy, scaled(at_z, lo))


def scatter_rows(arrived, group, size_xy, size_z):
    devices, fields, capacity = arrived.shape
    return pl.pallas_call(
        scatter_kernel,
        grid=(devices // group,),
        out_shape=jax.ShapeDtypeStruct((3, size_xy, size_z), F32),
        in_specs=[pl.BlockSpec((group, fields, capacity), lambda i: (i, 0, 0))],
        out_specs=pl.BlockSpec((3, size_xy, size_z), lambda i: (0, 0, 0)),
        name="scatter_rows",
    )(arrived)


def gather_kernel(arrived, field, boxes, terms):
    parts, size_xy, size_z = field.shape
    devices = boxes.shape[0]

    @pl.when(pl.program_id(0) == 0)
    def _():
        boxes[...] = jnp.zeros_like(boxes)
        for k in range(parts):
            hi, lo = two_terms(field[k].T)
            terms[k, :, :size_xy] = hi.astype(BF16)
            terms[k, :, size_xy:] = lo.astype(BF16)

    block = joined(arrived)
    at_z = matches(size_z, block[4:5].astype(jnp.int32))
    at_xy = one_hot(matches(size_xy, block[5:6].astype(jnp.int32)))
    twice = jnp.concatenate([at_xy, at_xy], axis=0)
    at_owner = one_hot(matches(devices, block[6:7].astype(jnp.int32)))
    at_slot = matches(BOX_DEV, block[7:8].astype(jnp.int32))
    for k in range(parts):
        column = jnp.dot(terms[k], twice, preferred_element_type=F32)
        value = jnp.sum(jnp.where(at_z, column, 0.0), axis=0, keepdims=True) * block[3:4]
        hi, lo = two_terms(value)
        part = dot_nt(at_owner, scaled(at_slot, hi)) + dot_nt(at_owner, scaled(at_slot, lo))
        boxes[:, k * BOX_DEV : (k + 1) * BOX_DEV] += part


def gather_rows(arrived, group, field):
    devices, fields, capacity = arrived.shape
    parts, size_xy, size_z = field.shape
    return pl.pallas_call(
        gather_kernel,
        grid=(devices // group,),
        out_shape=jax.ShapeDtypeStruct((devices, 3 * BOX_DEV), F32),
        in_specs=[
            pl.BlockSpec((group, fields, capacity), lambda i: (i, 0, 0)),
            pl.BlockSpec(memory_space=pltpu.VMEM),
        ],
        out_specs=pl.BlockSpec((devices, 3 * BOX_DEV), lambda i: (0, 0)),
        scratch_shapes=[pltpu.VMEM((parts, size_z, 2 * size_xy), BF16)],
        name="gather_rows",
    )(arrived, field)


def sweep_kernel(load, stiff, anchor, coupling, adjoint, weighted, rest, inverse, edge, halo, x_send, x_recv, y_send, y_recv):
    parts, size_x, size_y, size_z = load.shape
    exchanges = weighted.shape[0]
    gx, gy = lax.axis_index("gx"), lax.axis_index("gy")
    last_x, last_y = lax.axis_size("gx") - 1, lax.axis_size("gy") - 1
    sides = (("gx", gx, -1, gx > 0), ("gx", gx, 1, gx < last_x), ("gy", gy, -1, gy > 0), ("gy", gy, 1, gy < last_y))
    y_at = lax.broadcasted_iota(jnp.int32, (size_y, size_z), 0)
    z_at = lax.broadcasted_iota(jnp.int32, (size_y, size_z), 1)

    for index in range(exchanges):
        for k in range(parts):
            weighted[index, k, 0] = jnp.zeros((size_y, size_z), F32)
            weighted[index, k, size_x + 1] = jnp.zeros((size_y, size_z), F32)
    halo[...] = jnp.zeros_like(halo)

    barrier = pltpu.get_barrier_semaphore()
    known = 0
    for axis, place, move, present in sides:
        known = known + present.astype(jnp.int32)

        @pl.when(present)
        def _():
            pl.semaphore_signal(barrier, inc=1, device_id={axis: place + move}, device_id_type=MESH)

    pl.semaphore_wait(barrier, known)

    def copies(index):
        made = []
        for side, (axis, place, move, present) in enumerate(sides):
            there = 1 - side % 2
            if axis == "gx":
                pair = (weighted.at[index, :, 1 if move < 0 else size_x], weighted.at[index, :, size_x + 1 if move < 0 else 0])
                sems = (x_send, x_recv)
            else:
                pair = (edge.at[index, side % 2], halo.at[index, there])
                sems = (y_send, y_recv)
            made.append((present, pltpu.make_async_remote_copy(
                src_ref=pair[0],
                dst_ref=pair[1],
                send_sem=sems[0].at[index, side % 2],
                recv_sem=sems[1].at[index, there],
                device_id={axis: place + move},
                device_id_type=MESH,
            )))
        return made

    def arrivals(index):
        made = []
        for side, (axis, place, move, present) in enumerate(sides):
            if axis == "gx":
                pair = (weighted.at[index, :, 1 if move < 0 else size_x], weighted.at[index, :, 0 if move < 0 else size_x + 1])
                sems = (x_send, x_recv)
            else:
                pair = (edge.at[index, side % 2], halo.at[index, side % 2])
                sems = (y_send, y_recv)
            made.append((present, pltpu.make_async_remote_copy(
                src_ref=pair[0],
                dst_ref=pair[1],
                send_sem=sems[0].at[index, side % 2],
                recv_sem=sems[1].at[index, side % 2],
                device_id={axis: place + move},
                device_id_type=MESH,
            )))
        return made

    def publish(index, x, k, value):
        adjoint[k, x] = value
        if index < exchanges:
            product = stiff[x] * value
            weighted[index, k, x + 1] = product
            edge[index, 0, k, pl.ds(x, 1), :] = product[0:1]
            edge[index, 1, k, pl.ds(x, 1), :] = product[size_y - 1 : size_y]

    def first(x, carry):
        for k in range(parts):
            inverse[k, x] = 1.0 / (6.0 * stiff[x] + anchor[k, x] + coupling[4 * k, x])
            publish(0, x, k, load[k, x] * inverse[k, x])
        return carry

    lax.fori_loop(0, size_x, first, 0)
    for index in range(exchanges):
        for present, copy in copies(index):

            @pl.when(present)
            def _():
                copy.start()

        def near(x, carry):
            fields = [adjoint[k, x] for k in range(parts)]
            for k in range(parts):
                product = weighted[index, k, x + 1]
                value = load[k, x] - 6.0 * product - anchor[k, x] * fields[k]
                for j in range(parts):
                    value = value - coupling[3 * j + k, x] * fields[j]
                value = value + jnp.where(z_at == 0, 0.0, pltpu.roll(product, 1, 1))
                value = value + jnp.where(z_at == size_z - 1, 0.0, pltpu.roll(product, size_z - 1, 1))
                value = value + jnp.where(y_at == 0, 0.0, pltpu.roll(product, 1, 0))
                value = value + jnp.where(y_at == size_y - 1, 0.0, pltpu.roll(product, size_y - 1, 0))
                rest[k, x] = value
            return carry

        lax.fori_loop(0, size_x, near, 0)
        for present, copy in arrivals(index):

            @pl.when(present)
            def _():
                copy.wait_recv()

        def far(x, carry):
            for k in range(parts):
                value = rest[k, x] + weighted[index, k, x] + weighted[index, k, x + 2]
                value = value + jnp.where(y_at == 0, halo[index, 0, k, pl.ds(x, 1), :], 0.0)
                value = value + jnp.where(y_at == size_y - 1, halo[index, 1, k, pl.ds(x, 1), :], 0.0)
                publish(index + 1, x, k, adjoint[k, x] + value * inverse[k, x])
            return carry

        lax.fori_loop(0, size_x, far, 0)
    for index in range(exchanges):
        for present, copy in copies(index):

            @pl.when(present)
            def _():
                copy.wait_send()


def solve_sweeps(load, stiffness, anchor, coupling):
    parts, size_x, size_y, size_z = load.shape
    exchanges = SWEEPS - 1
    return pl.pallas_call(
        sweep_kernel,
        out_shape=jax.ShapeDtypeStruct(load.shape, F32),
        in_specs=[pl.BlockSpec(memory_space=pltpu.VMEM)] * 4,
        out_specs=pl.BlockSpec(memory_space=pltpu.VMEM),
        scratch_shapes=[
            pltpu.VMEM((exchanges, parts, size_x + 2, size_y, size_z), F32),
            pltpu.VMEM(load.shape, F32),
            pltpu.VMEM(load.shape, F32),
            pltpu.VMEM((exchanges, 2, parts, size_x, size_z), F32),
            pltpu.VMEM((exchanges, 2, parts, size_x, size_z), F32),
        ]
        + [pltpu.SemaphoreType.DMA((exchanges, 2))] * 4,
        compiler_params=pltpu.CompilerParams(collective_id=0, has_side_effects=True),
        name="sweeps",
    )(load, stiffness, anchor, coupling)


def body(
    sensitivity,
    node_weight,
    dest_device,
    dest_cell,
    box_owner,
    box_slot,
    stiffness,
    anchor,
    coupling,
):
    devices = lax.axis_size("gx") * lax.axis_size("gy")
    row_count = sensitivity.shape[1]
    capacity = 2 * row_count // devices
    size_x, size_y, size_z = stiffness.shape
    size_xy = size_x * size_y
    group = max(1, min(devices, 512 // capacity))

    def row(values):
        return values.reshape(1, row_count)

    packed = pack_rows(
        size_z,
        devices,
        capacity,
        sensitivity,
        row(node_weight),
        row(dest_device),
        row(dest_cell),
        row(box_owner),
        row(box_slot),
    )
    arrived = lax.all_to_all(packed, ("gx", "gy"), split_axis=0, concat_axis=0, tiled=True)
    load = scatter_rows(arrived, group, size_xy, size_z)
    load = load.reshape(3, size_x, size_y, size_z)
    adjoint = solve_sweeps(load, stiffness, anchor, coupling)
    partial = gather_rows(arrived, group, adjoint.reshape(3, size_xy, size_z))
    partial = lax.all_to_all(partial, ("gx", "gy"), split_axis=0, concat_axis=0, tiled=True)
    box_gradient = jnp.sum(partial, axis=0).reshape(3, BOX_DEV)
    return (adjoint, box_gradient)


def solution(mesh):
    placed = (
        P(None, ("gx", "gy")),
        P(("gx", "gy")),
        P(("gx", "gy"), None),
        P(("gx", "gy")),
        P(("gx", "gy"), None),
        P(("gx", "gy")),
        P("gx", "gy", None),
        P(None, "gx", "gy", None),
        P(None, "gx", "gy", None),
    )
    return jax.shard_map(
        body,
        mesh=mesh,
        in_specs=placed,
        out_specs=(P(None, "gx", "gy", None), P(None, ("gx", "gy"))),
        check_vma=False,
    )
```

```python
import functools

import jax
import jax.numpy as jnp
from jax import lax
from jax.experimental import pallas as pl
from jax.experimental.pallas import tpu as pltpu
from jax.sharding import PartitionSpec as P

BOX_DEV = 64
SWEEPS = 4
NT = (((1,), (1,)), ((), ()))
F32 = jnp.float32
BF16 = jnp.bfloat16
MESH = pl.DeviceIdType.MESH


def two_terms(x):
    hi = x.astype(BF16).astype(F32)
    return hi, x - hi


def matches(count, row):
    return lax.broadcasted_iota(jnp.int32, (count, row.shape[1]), 0) == row


def one_hot(mask):
    return jnp.where(mask, 1.0, 0.0).astype(BF16)


def scaled(mask, row):
    return jnp.where(mask, row, 0.0).astype(BF16)


def dot_nt(a, b):
    return lax.dot_general(a, b, NT, preferred_element_type=F32)


def pack_kernel(size_z, step, sens, weight, device, cell, owner, slot, out, tri, seen):
    targets, fields, capacity = out.shape
    rows = sens.shape[1]
    out[...] = jnp.zeros_like(out)
    seen[...] = jnp.zeros_like(seen)
    tri[...] = one_hot(
        lax.broadcasted_iota(jnp.int32, (step, step), 0)
        < lax.broadcasted_iota(jnp.int32, (step, step), 1)
    )

    def block(index, carry):
        span = pl.ds(pl.multiple_of(index * step, step), step)
        target = device[:, span]
        chosen = matches(targets, target)
        before = jnp.dot(one_hot(chosen), tri[...], preferred_element_type=F32) + seen[:, :1]
        rank = jnp.sum(jnp.where(chosen, before, 0.0), axis=0, keepdims=True).astype(jnp.int32)
        seen[...] = seen[...] + jnp.sum(jnp.where(chosen, 1.0, 0.0), axis=1, keepdims=True)
        place = one_hot(matches(capacity, rank))
        cells = cell[:, span]
        payload = jnp.concatenate(
            [
                sens[:, span],
                weight[:, span],
                (cells % size_z).astype(F32),
                (cells // size_z).astype(F32),
                owner[:, span].astype(F32),
                slot[:, span].astype(F32),
            ],
            axis=0,
        )
        wide = (targets, fields, step)
        to = lax.broadcasted_iota(jnp.int32, wide, 0) == target[None]
        terms = [
            jnp.where(to, term[None], 0.0).reshape(targets * fields, step).astype(BF16)
            for term in two_terms(payload)
        ]
        product = dot_nt(jnp.concatenate(terms, axis=0), place)
        product = product[: targets * fields] + product[targets * fields :]
        out[...] = out[...] + product.reshape(targets, fields, capacity)
        return carry

    lax.fori_loop(0, rows // step, block, 0)


def pack_rows(size_z, devices, capacity, sens, weight, device, cell, owner, slot):
    step = min(512, sens.shape[1])
    return pl.pallas_call(
        functools.partial(pack_kernel, size_z, step),
        out_shape=jax.ShapeDtypeStruct((devices, 8, capacity), F32),
        in_specs=[pl.BlockSpec(memory_space=pltpu.VMEM)] * 6,
        out_specs=pl.BlockSpec(memory_space=pltpu.VMEM),
        scratch_shapes=[pltpu.VMEM((step, step), BF16), pltpu.VMEM((devices, 128), F32)],
        name="pack_rows",
    )(sens, weight, device, cell, owner, slot)


def joined(ref):
    return jnp.concatenate([ref[i] for i in range(ref.shape[0])], axis=1)


def scatter_kernel(arrived, load, total):
    parts, size_xy, size_z = load.shape

    @pl.when(pl.program_id(0) == 0)
    def _():
        total[...] = jnp.zeros_like(total)

    block = joined(arrived)
    at_z = matches(size_z, block[4:5].astype(jnp.int32))
    at_xy = one_hot(matches(size_xy, block[5:6].astype(jnp.int32)))
    pairs = [two_terms(block[k : k + 1]) for k in range(parts)]
    terms = [scaled(at_z, hi) for hi, lo in pairs] + [scaled(at_z, lo) for hi, lo in pairs]
    product = dot_nt(jnp.concatenate(terms, axis=0), at_xy)
    half = parts * size_z
    total[...] = total[...] + product[:half] + product[half:]

    @pl.when(pl.program_id(0) == pl.num_programs(0) - 1)
    def _():
        for k in range(parts):
            load[k] = total[k * size_z : (k + 1) * size_z].T


def scatter_rows(arrived, group, size_xy, size_z):
    devices, fields, capacity = arrived.shape
    return pl.pallas_call(
        scatter_kernel,
        grid=(devices // group,),
        out_shape=jax.ShapeDtypeStruct((3, size_xy, size_z), F32),
        in_specs=[pl.BlockSpec((group, fields, capacity), lambda i: (i, 0, 0))],
        out_specs=pl.BlockSpec((3, size_xy, size_z), lambda i: (0, 0, 0)),
        scratch_shapes=[pltpu.VMEM((3 * size_z, size_xy), F32)],
        name="scatter_rows",
    )(arrived)


def gather_kernel(arrived, field, boxes, terms):
    parts, size_xy, size_z = field.shape
    devices = boxes.shape[0]

    @pl.when(pl.program_id(0) == 0)
    def _():
        boxes[...] = jnp.zeros_like(boxes)
        for k in range(parts):
            hi, lo = two_terms(field[k].T)
            terms[k * size_z : (k + 1) * size_z] = hi.astype(BF16)
            terms[(parts + k) * size_z : (parts + k + 1) * size_z] = lo.astype(BF16)

    block = joined(arrived)
    at_z = matches(size_z, block[4:5].astype(jnp.int32))
    at_xy = one_hot(matches(size_xy, block[5:6].astype(jnp.int32)))
    columns = jnp.dot(terms[...], at_xy, preferred_element_type=F32)
    at_owner = one_hot(matches(devices, block[6:7].astype(jnp.int32)))
    at_slot = matches(BOX_DEV, block[7:8].astype(jnp.int32))
    for k in range(parts):
        column = columns[k * size_z : (k + 1) * size_z]
        column = column + columns[(parts + k) * size_z : (parts + k + 1) * size_z]
        value = jnp.sum(jnp.where(at_z, column, 0.0), axis=0, keepdims=True) * block[3:4]
        hi, lo = two_terms(value)
        part = dot_nt(at_owner, scaled(at_slot, hi)) + dot_nt(at_owner, scaled(at_slot, lo))
        boxes[:, k * BOX_DEV : (k + 1) * BOX_DEV] += part


def gather_rows(arrived, group, field):
    devices, fields, capacity = arrived.shape
    parts, size_xy, size_z = field.shape
    return pl.pallas_call(
        gather_kernel,
        grid=(devices // group,),
        out_shape=jax.ShapeDtypeStruct((devices, 3 * BOX_DEV), F32),
        in_specs=[
            pl.BlockSpec((group, fields, capacity), lambda i: (i, 0, 0)),
            pl.BlockSpec(memory_space=pltpu.VMEM),
        ],
        out_specs=pl.BlockSpec((devices, 3 * BOX_DEV), lambda i: (0, 0)),
        scratch_shapes=[pltpu.VMEM((2 * parts * size_z, size_xy), BF16)],
        name="gather_rows",
    )(arrived, field)


def sweep_kernel(load, stiff, anchor, coupling, adjoint, weighted, rest, inverse, edge, halo, x_send, x_recv, y_send, y_recv):
    parts, size_x, size_y, size_z = load.shape
    exchanges = weighted.shape[0]
    gx, gy = lax.axis_index("gx"), lax.axis_index("gy")
    last_x, last_y = lax.axis_size("gx") - 1, lax.axis_size("gy") - 1
    sides = (("gx", gx, -1, gx > 0), ("gx", gx, 1, gx < last_x), ("gy", gy, -1, gy > 0), ("gy", gy, 1, gy < last_y))
    y_at = lax.broadcasted_iota(jnp.int32, (size_y, size_z), 0)
    z_at = lax.broadcasted_iota(jnp.int32, (size_y, size_z), 1)

    for index in range(exchanges):
        for k in range(parts):
            weighted[index, k, 0] = jnp.zeros((size_y, size_z), F32)
            weighted[index, k, size_x + 1] = jnp.zeros((size_y, size_z), F32)
    halo[...] = jnp.zeros_like(halo)

    barrier = pltpu.get_barrier_semaphore()
    known = 0
    for axis, place, move, present in sides:
        known = known + present.astype(jnp.int32)

        @pl.when(present)
        def _():
            pl.semaphore_signal(barrier, inc=1, device_id={axis: place + move}, device_id_type=MESH)

    pl.semaphore_wait(barrier, known)

    def copies(index):
        made = []
        for side, (axis, place, move, present) in enumerate(sides):
            there = 1 - side % 2
            if axis == "gx":
                pair = (weighted.at[index, :, 1 if move < 0 else size_x], weighted.at[index, :, size_x + 1 if move < 0 else 0])
                sems = (x_send, x_recv)
            else:
                pair = (edge.at[index, side % 2], halo.at[index, there])
                sems = (y_send, y_recv)
            made.append((present, pltpu.make_async_remote_copy(
                src_ref=pair[0],
                dst_ref=pair[1],
                send_sem=sems[0].at[index, side % 2],
                recv_sem=sems[1].at[index, there],
                device_id={axis: place + move},
                device_id_type=MESH,
            )))
        return made

    def arrivals(index):
        made = []
        for side, (axis, place, move, present) in enumerate(sides):
            if axis == "gx":
                pair = (weighted.at[index, :, 1 if move < 0 else size_x], weighted.at[index, :, 0 if move < 0 else size_x + 1])
                sems = (x_send, x_recv)
            else:
                pair = (edge.at[index, side % 2], halo.at[index, side % 2])
                sems = (y_send, y_recv)
            made.append((present, pltpu.make_async_remote_copy(
                src_ref=pair[0],
                dst_ref=pair[1],
                send_sem=sems[0].at[index, side % 2],
                recv_sem=sems[1].at[index, side % 2],
                device_id={axis: place + move},
                device_id_type=MESH,
            )))
        return made

    def publish(index, x, k, value):
        adjoint[k, x] = value
        if index < exchanges:
            product = stiff[x] * value
            weighted[index, k, x + 1] = product
            edge[index, 0, k, pl.ds(x, 1), :] = product[0:1]
            edge[index, 1, k, pl.ds(x, 1), :] = product[size_y - 1 : size_y]

    def first(x, carry):
        for k in range(parts):
            inverse[k, x] = 1.0 / (6.0 * stiff[x] + anchor[k, x] + coupling[4 * k, x])
            publish(0, x, k, load[k, x] * inverse[k, x])
        return carry

    lax.fori_loop(0, size_x, first, 0)
    for index in range(exchanges):
        for present, copy in copies(index):

            @pl.when(present)
            def _():
                copy.start()

        def near(x, carry):
            fields = [adjoint[k, x] for k in range(parts)]
            for k in range(parts):
                product = weighted[index, k, x + 1]
                value = load[k, x] - 6.0 * product - anchor[k, x] * fields[k]
                for j in range(parts):
                    value = value - coupling[3 * j + k, x] * fields[j]
                value = value + jnp.where(z_at == 0, 0.0, pltpu.roll(product, 1, 1))
                value = value + jnp.where(z_at == size_z - 1, 0.0, pltpu.roll(product, size_z - 1, 1))
                value = value + jnp.where(y_at == 0, 0.0, pltpu.roll(product, 1, 0))
                value = value + jnp.where(y_at == size_y - 1, 0.0, pltpu.roll(product, size_y - 1, 0))
                rest[k, x] = value
            return carry

        lax.fori_loop(0, size_x, near, 0)
        for present, copy in arrivals(index):

            @pl.when(present)
            def _():
                copy.wait_recv()

        def far(x, carry):
            for k in range(parts):
                value = rest[k, x] + weighted[index, k, x] + weighted[index, k, x + 2]
                value = value + jnp.where(y_at == 0, halo[index, 0, k, pl.ds(x, 1), :], 0.0)
                value = value + jnp.where(y_at == size_y - 1, halo[index, 1, k, pl.ds(x, 1), :], 0.0)
                publish(index + 1, x, k, adjoint[k, x] + value * inverse[k, x])
            return carry

        lax.fori_loop(0, size_x, far, 0)
    for index in range(exchanges):
        for present, copy in copies(index):

            @pl.when(present)
            def _():
                copy.wait_send()


def solve_sweeps(load, stiffness, anchor, coupling):
    parts, size_x, size_y, size_z = load.shape
    exchanges = SWEEPS - 1
    return pl.pallas_call(
        sweep_kernel,
        out_shape=jax.ShapeDtypeStruct(load.shape, F32),
        in_specs=[pl.BlockSpec(memory_space=pltpu.VMEM)] * 4,
        out_specs=pl.BlockSpec(memory_space=pltpu.VMEM),
        scratch_shapes=[
            pltpu.VMEM((exchanges, parts, size_x + 2, size_y, size_z), F32),
            pltpu.VMEM(load.shape, F32),
            pltpu.VMEM(load.shape, F32),
            pltpu.VMEM((exchanges, 2, parts, size_x, size_z), F32),
            pltpu.VMEM((exchanges, 2, parts, size_x, size_z), F32),
        ]
        + [pltpu.SemaphoreType.DMA((exchanges, 2))] * 4,
        compiler_params=pltpu.CompilerParams(collective_id=0, has_side_effects=True),
        name="sweeps",
    )(load, stiffness, anchor, coupling)


def exchange_kernel(send, recv, send_sem, recv_sem, own_sem):
    count = send.shape[0]
    width = lax.axis_size("gy")
    me = lax.axis_index("gx") * width + lax.axis_index("gy")
    barrier = pltpu.get_barrier_semaphore()

    def device(index):
        return (index // width, index % width)

    def greet(step, carry):
        pl.semaphore_signal(barrier, inc=1, device_id=device((me + step) % count), device_id_type=MESH)
        return carry

    lax.fori_loop(1, count, greet, 0)
    pl.semaphore_wait(barrier, count - 1)

    def copy(step, source, landing):
        peer = (me + step) % count
        return pltpu.make_async_remote_copy(
            src_ref=send.at[source],
            dst_ref=recv.at[landing],
            send_sem=send_sem.at[step],
            recv_sem=recv_sem.at[step],
            device_id=device(peer),
            device_id_type=MESH,
        )

    def start(step, carry):
        copy(step, (me + step) % count, me).start()
        return carry

    lax.fori_loop(1, count, start, 0)
    own = pltpu.make_async_copy(send.at[me], recv.at[me], own_sem)
    own.start()

    def finish(step, carry):
        copy(step, (me + step) % count, (me + count - step) % count).wait_recv()
        copy(step, (me + step) % count, me).wait_send()
        return carry

    lax.fori_loop(1, count, finish, 0)
    own.wait()


def exchange(blocks, number):
    count = blocks.shape[0]
    return pl.pallas_call(
        exchange_kernel,
        out_shape=jax.ShapeDtypeStruct(blocks.shape, F32),
        in_specs=[pl.BlockSpec(memory_space=pltpu.VMEM)],
        out_specs=pl.BlockSpec(memory_space=pltpu.VMEM),
        scratch_shapes=[pltpu.SemaphoreType.DMA((count,))] * 2 + [pltpu.SemaphoreType.DMA],
        compiler_params=pltpu.CompilerParams(collective_id=number, has_side_effects=True),
        name="exchange_" + str(number),
    )(blocks)


def body(
    sensitivity,
    node_weight,
    dest_device,
    dest_cell,
    box_owner,
    box_slot,
    stiffness,
    anchor,
    coupling,
):
    devices = lax.axis_size("gx") * lax.axis_size("gy")
    row_count = sensitivity.shape[1]
    capacity = 2 * row_count // devices
    size_x, size_y, size_z = stiffness.shape
    size_xy = size_x * size_y
    group = max(1, min(devices, 512 // capacity))

    def row(values):
        return values.reshape(1, row_count)

    packed = pack_rows(
        size_z,
        devices,
        capacity,
        sensitivity,
        row(node_weight),
        row(dest_device),
        row(dest_cell),
        row(box_owner),
        row(box_slot),
    )
    arrived = exchange(packed, 1)
    load = scatter_rows(arrived, group, size_xy, size_z)
    load = load.reshape(3, size_x, size_y, size_z)
    adjoint = solve_sweeps(load, stiffness, anchor, coupling)
    partial = gather_rows(arrived, group, adjoint.reshape(3, size_xy, size_z))
    partial = exchange(partial.reshape(devices, 1, 3 * BOX_DEV), 2)
    box_gradient = jnp.sum(partial, axis=(0, 1)).reshape(3, BOX_DEV)
    return (adjoint, box_gradient)


def solution(mesh):
    placed = (
        P(None, ("gx", "gy")),
        P(("gx", "gy")),
        P(("gx", "gy"), None),
        P(("gx", "gy")),
        P(("gx", "gy"), None),
        P(("gx", "gy")),
        P("gx", "gy", None),
        P(None, "gx", "gy", None),
        P(None, "gx", "gy", None),
    )
    return jax.shard_map(
        body,
        mesh=mesh,
        in_specs=placed,
        out_specs=(P(None, "gx", "gy", None), P(None, ("gx", "gy"))),
        check_vma=False,
    )
```

```python
import functools

import jax
import jax.numpy as jnp
from jax import lax
from jax.experimental import pallas as pl
from jax.experimental.pallas import tpu as pltpu
from jax.sharding import PartitionSpec as P

BOX_DEV = 64
SWEEPS = 4
SENT = 6
NT = (((1,), (1,)), ((), ()))
F32 = jnp.float32
BF16 = jnp.bfloat16
MESH = pl.DeviceIdType.MESH


def two_terms(x):
    hi = x.astype(BF16).astype(F32)
    return hi, x - hi


def matches(count, row):
    return lax.broadcasted_iota(jnp.int32, (count, row.shape[1]), 0) == row


def one_hot(mask):
    return jnp.where(mask, 1.0, 0.0).astype(BF16)


def scaled(mask, row):
    return jnp.where(mask, row, 0.0).astype(BF16)


def dot_nt(a, b):
    return lax.dot_general(a, b, NT, preferred_element_type=F32)


def pack_kernel(step, sens, weight, device, cell, owner, slot, out, tri, seen):
    targets, fields, capacity = out.shape
    rows = sens.shape[1]
    out[...] = jnp.zeros_like(out)
    seen[...] = jnp.zeros_like(seen)
    tri[...] = one_hot(
        lax.broadcasted_iota(jnp.int32, (step, step), 0)
        < lax.broadcasted_iota(jnp.int32, (step, step), 1)
    )

    def block(index, carry):
        span = pl.ds(pl.multiple_of(index * step, step), step)
        target = device[:, span]
        chosen = matches(targets, target)
        before = jnp.dot(one_hot(chosen), tri[...], preferred_element_type=F32) + seen[:, :1]
        rank = jnp.sum(jnp.where(chosen, before, 0.0), axis=0, keepdims=True).astype(jnp.int32)
        seen[...] = seen[...] + jnp.sum(jnp.where(chosen, 1.0, 0.0), axis=1, keepdims=True)
        place = one_hot(matches(capacity, rank))
        payload = jnp.concatenate(
            [
                sens[:, span],
                cell[:, span].astype(F32),
                weight[:, span],
                (owner[:, span] * BOX_DEV + slot[:, span]).astype(F32),
                jnp.zeros((fields - SENT, step), F32),
            ],
            axis=0,
        )
        wide = (targets, fields, step)
        to = lax.broadcasted_iota(jnp.int32, wide, 0) == target[None]
        terms = [
            jnp.where(to, term[None], 0.0).reshape(targets * fields, step).astype(BF16)
            for term in two_terms(payload)
        ]
        product = dot_nt(jnp.concatenate(terms, axis=0), place)
        product = product[: targets * fields] + product[targets * fields :]
        out[...] = out[...] + product.reshape(targets, fields, capacity)
        return carry

    lax.fori_loop(0, rows // step, block, 0)


def pack_rows(devices, capacity, sens, weight, device, cell, owner, slot):
    step = min(1024, sens.shape[1])
    return pl.pallas_call(
        functools.partial(pack_kernel, step),
        out_shape=jax.ShapeDtypeStruct((devices, 8, capacity), F32),
        in_specs=[pl.BlockSpec(memory_space=pltpu.VMEM)] * 6,
        out_specs=pl.BlockSpec(memory_space=pltpu.VMEM),
        scratch_shapes=[pltpu.VMEM((step, step), BF16), pltpu.VMEM((devices, 128), F32)],
        name="pack_rows",
    )(sens, weight, device, cell, owner, slot)


def joined(ref):
    return jnp.concatenate([ref[i, :SENT] for i in range(ref.shape[0])], axis=1)


def scatter_kernel(arrived, load, total):
    parts, size_xy, size_z = load.shape

    @pl.when(pl.program_id(0) == 0)
    def _():
        total[...] = jnp.zeros_like(total)

    block = joined(arrived)
    cell = block[3:4].astype(jnp.int32)
    at_z = matches(size_z, cell % size_z)
    at_xy = one_hot(matches(size_xy, cell // size_z))
    pairs = [two_terms(block[k : k + 1]) for k in range(parts)]
    terms = [scaled(at_z, hi) for hi, lo in pairs] + [scaled(at_z, lo) for hi, lo in pairs]
    product = dot_nt(jnp.concatenate(terms, axis=0), at_xy)
    half = parts * size_z
    total[...] = total[...] + product[:half] + product[half:]

    @pl.when(pl.program_id(0) == pl.num_programs(0) - 1)
    def _():
        for k in range(parts):
            load[k] = total[k * size_z : (k + 1) * size_z].T


def scatter_rows(arrived, group, size_xy, size_z):
    devices, fields, capacity = arrived.shape
    return pl.pallas_call(
        scatter_kernel,
        grid=(devices // group,),
        out_shape=jax.ShapeDtypeStruct((3, size_xy, size_z), F32),
        in_specs=[pl.BlockSpec((group, fields, capacity), lambda i: (i, 0, 0))],
        out_specs=pl.BlockSpec((3, size_xy, size_z), lambda i: (0, 0, 0)),
        scratch_shapes=[pltpu.VMEM((3 * size_z, size_xy), F32)],
        name="scatter_rows",
    )(arrived)


def gather_kernel(arrived, field, boxes, terms):
    parts, size_xy, size_z = field.shape
    devices = boxes.shape[0]

    @pl.when(pl.program_id(0) == 0)
    def _():
        boxes[...] = jnp.zeros_like(boxes)
        for k in range(parts):
            hi, lo = two_terms(field[k].T)
            terms[k * size_z : (k + 1) * size_z] = hi.astype(BF16)
            terms[(parts + k) * size_z : (parts + k + 1) * size_z] = lo.astype(BF16)

    block = joined(arrived)
    cell = block[3:4].astype(jnp.int32)
    at_z = matches(size_z, cell % size_z)
    at_xy = one_hot(matches(size_xy, cell // size_z))
    columns = jnp.dot(terms[...], at_xy, preferred_element_type=F32)
    box = block[5:6].astype(jnp.int32)
    at_owner = one_hot(matches(devices, box // BOX_DEV))
    at_slot = matches(BOX_DEV, box % BOX_DEV)
    for k in range(parts):
        column = columns[k * size_z : (k + 1) * size_z]
        column = column + columns[(parts + k) * size_z : (parts + k + 1) * size_z]
        value = jnp.sum(jnp.where(at_z, column, 0.0), axis=0, keepdims=True) * block[4:5]
        hi, lo = two_terms(value)
        part = dot_nt(at_owner, scaled(at_slot, hi)) + dot_nt(at_owner, scaled(at_slot, lo))
        boxes[:, k * BOX_DEV : (k + 1) * BOX_DEV] += part


def gather_rows(arrived, group, field):
    devices, fields, capacity = arrived.shape
    parts, size_xy, size_z = field.shape
    return pl.pallas_call(
        gather_kernel,
        grid=(devices // group,),
        out_shape=jax.ShapeDtypeStruct((devices, 3 * BOX_DEV), F32),
        in_specs=[
            pl.BlockSpec((group, fields, capacity), lambda i: (i, 0, 0)),
            pl.BlockSpec(memory_space=pltpu.VMEM),
        ],
        out_specs=pl.BlockSpec((devices, 3 * BOX_DEV), lambda i: (0, 0)),
        scratch_shapes=[pltpu.VMEM((2 * parts * size_z, size_xy), BF16)],
        name="gather_rows",
    )(arrived, field)


def sweep_kernel(load, stiff, anchor, coupling, adjoint, weighted, rest, inverse, edge, halo, x_send, x_recv, y_send, y_recv):
    parts, size_x, size_y, size_z = load.shape
    exchanges = weighted.shape[0]
    gx, gy = lax.axis_index("gx"), lax.axis_index("gy")
    last_x, last_y = lax.axis_size("gx") - 1, lax.axis_size("gy") - 1
    sides = (("gx", gx, -1, gx > 0), ("gx", gx, 1, gx < last_x), ("gy", gy, -1, gy > 0), ("gy", gy, 1, gy < last_y))
    y_at = lax.broadcasted_iota(jnp.int32, (size_y, size_z), 0)
    z_at = lax.broadcasted_iota(jnp.int32, (size_y, size_z), 1)

    for index in range(exchanges):
        for k in range(parts):
            weighted[index, k, 0] = jnp.zeros((size_y, size_z), F32)
            weighted[index, k, size_x + 1] = jnp.zeros((size_y, size_z), F32)
    halo[...] = jnp.zeros_like(halo)

    barrier = pltpu.get_barrier_semaphore()
    known = 0
    for axis, place, move, present in sides:
        known = known + present.astype(jnp.int32)

        @pl.when(present)
        def _():
            pl.semaphore_signal(barrier, inc=1, device_id={axis: place + move}, device_id_type=MESH)

    pl.semaphore_wait(barrier, known)

    def copies(index):
        made = []
        for side, (axis, place, move, present) in enumerate(sides):
            there = 1 - side % 2
            if axis == "gx":
                pair = (weighted.at[index, :, 1 if move < 0 else size_x], weighted.at[index, :, size_x + 1 if move < 0 else 0])
                sems = (x_send, x_recv)
            else:
                pair = (edge.at[index, side % 2], halo.at[index, there])
                sems = (y_send, y_recv)
            made.append((present, pltpu.make_async_remote_copy(
                src_ref=pair[0],
                dst_ref=pair[1],
                send_sem=sems[0].at[index, side % 2],
                recv_sem=sems[1].at[index, there],
                device_id={axis: place + move},
                device_id_type=MESH,
            )))
        return made

    def arrivals(index):
        made = []
        for side, (axis, place, move, present) in enumerate(sides):
            if axis == "gx":
                pair = (weighted.at[index, :, 1 if move < 0 else size_x], weighted.at[index, :, 0 if move < 0 else size_x + 1])
                sems = (x_send, x_recv)
            else:
                pair = (edge.at[index, side % 2], halo.at[index, side % 2])
                sems = (y_send, y_recv)
            made.append((present, pltpu.make_async_remote_copy(
                src_ref=pair[0],
                dst_ref=pair[1],
                send_sem=sems[0].at[index, side % 2],
                recv_sem=sems[1].at[index, side % 2],
                device_id={axis: place + move},
                device_id_type=MESH,
            )))
        return made

    def publish(index, x, k, value):
        adjoint[k, x] = value
        if index < exchanges:
            product = stiff[x] * value
            weighted[index, k, x + 1] = product
            edge[index, 0, k, pl.ds(x, 1), :] = product[0:1]
            edge[index, 1, k, pl.ds(x, 1), :] = product[size_y - 1 : size_y]

    def first(x, carry):
        for k in range(parts):
            inverse[k, x] = 1.0 / (6.0 * stiff[x] + anchor[k, x] + coupling[4 * k, x])
            publish(0, x, k, load[k, x] * inverse[k, x])
        return carry

    lax.fori_loop(0, size_x, first, 0)
    for index in range(exchanges):
        for present, copy in copies(index):

            @pl.when(present)
            def _():
                copy.start()

        def near(x, carry):
            fields = [adjoint[k, x] for k in range(parts)]
            for k in range(parts):
                product = weighted[index, k, x + 1]
                value = load[k, x] - 6.0 * product - anchor[k, x] * fields[k]
                for j in range(parts):
                    value = value - coupling[3 * j + k, x] * fields[j]
                value = value + jnp.where(z_at == 0, 0.0, pltpu.roll(product, 1, 1))
                value = value + jnp.where(z_at == size_z - 1, 0.0, pltpu.roll(product, size_z - 1, 1))
                value = value + jnp.where(y_at == 0, 0.0, pltpu.roll(product, 1, 0))
                value = value + jnp.where(y_at == size_y - 1, 0.0, pltpu.roll(product, size_y - 1, 0))
                rest[k, x] = value
            return carry

        lax.fori_loop(0, size_x, near, 0)
        for present, copy in arrivals(index):

            @pl.when(present)
            def _():
                copy.wait_recv()

        def far(x, carry):
            for k in range(parts):
                value = rest[k, x] + weighted[index, k, x] + weighted[index, k, x + 2]
                value = value + jnp.where(y_at == 0, halo[index, 0, k, pl.ds(x, 1), :], 0.0)
                value = value + jnp.where(y_at == size_y - 1, halo[index, 1, k, pl.ds(x, 1), :], 0.0)
                publish(index + 1, x, k, adjoint[k, x] + value * inverse[k, x])
            return carry

        lax.fori_loop(0, size_x, far, 0)
    for index in range(exchanges):
        for present, copy in copies(index):

            @pl.when(present)
            def _():
                copy.wait_send()


def solve_sweeps(load, stiffness, anchor, coupling):
    parts, size_x, size_y, size_z = load.shape
    exchanges = SWEEPS - 1
    return pl.pallas_call(
        sweep_kernel,
        out_shape=jax.ShapeDtypeStruct(load.shape, F32),
        in_specs=[pl.BlockSpec(memory_space=pltpu.VMEM)] * 4,
        out_specs=pl.BlockSpec(memory_space=pltpu.VMEM),
        scratch_shapes=[
            pltpu.VMEM((exchanges, parts, size_x + 2, size_y, size_z), F32),
            pltpu.VMEM(load.shape, F32),
            pltpu.VMEM(load.shape, F32),
            pltpu.VMEM((exchanges, 2, parts, size_x, size_z), F32),
            pltpu.VMEM((exchanges, 2, parts, size_x, size_z), F32),
        ]
        + [pltpu.SemaphoreType.DMA((exchanges, 2))] * 4,
        compiler_params=pltpu.CompilerParams(collective_id=0, has_side_effects=True),
        name="sweeps",
    )(load, stiffness, anchor, coupling)


def exchange_kernel(live, send, recv, send_sem, recv_sem, own_sem):
    count = send.shape[0]
    width = lax.axis_size("gy")
    me = lax.axis_index("gx") * width + lax.axis_index("gy")
    barrier = pltpu.get_barrier_semaphore()

    def device(index):
        return (index // width, index % width)

    def greet(step, carry):
        pl.semaphore_signal(barrier, inc=1, device_id=device((me + step) % count), device_id_type=MESH)
        return carry

    lax.fori_loop(1, count, greet, 0)
    pl.semaphore_wait(barrier, count - 1)

    def copy(step, source, landing):
        peer = (me + step) % count
        return pltpu.make_async_remote_copy(
            src_ref=send.at[source, pl.ds(0, live)],
            dst_ref=recv.at[landing, pl.ds(0, live)],
            send_sem=send_sem.at[step],
            recv_sem=recv_sem.at[step],
            device_id=device(peer),
            device_id_type=MESH,
        )

    def start(step, carry):
        copy(step, (me + step) % count, me).start()
        return carry

    lax.fori_loop(1, count, start, 0)
    own = pltpu.make_async_copy(send.at[me, pl.ds(0, live)], recv.at[me, pl.ds(0, live)], own_sem)
    own.start()

    def finish(step, carry):
        copy(step, (me + step) % count, (me + count - step) % count).wait_recv()
        copy(step, (me + step) % count, me).wait_send()
        return carry

    lax.fori_loop(1, count, finish, 0)
    own.wait()


def exchange(blocks, live, number):
    count = blocks.shape[0]
    return pl.pallas_call(
        functools.partial(exchange_kernel, live),
        out_shape=jax.ShapeDtypeStruct(blocks.shape, F32),
        in_specs=[pl.BlockSpec(memory_space=pltpu.VMEM)],
        out_specs=pl.BlockSpec(memory_space=pltpu.VMEM),
        scratch_shapes=[pltpu.SemaphoreType.DMA((count,))] * 2 + [pltpu.SemaphoreType.DMA],
        compiler_params=pltpu.CompilerParams(collective_id=number, has_side_effects=True),
        name="exchange_" + str(number),
    )(blocks)


def body(
    sensitivity,
    node_weight,
    dest_device,
    dest_cell,
    box_owner,
    box_slot,
    stiffness,
    anchor,
    coupling,
):
    devices = lax.axis_size("gx") * lax.axis_size("gy")
    row_count = sensitivity.shape[1]
    capacity = 2 * row_count // devices
    size_x, size_y, size_z = stiffness.shape
    size_xy = size_x * size_y
    assert size_xy * size_z <= 2**17 and devices * BOX_DEV <= 2**17
    group = max(1, min(devices, 1024 // capacity))

    def row(values):
        return values.reshape(1, row_count)

    packed = pack_rows(
        devices,
        capacity,
        sensitivity,
        row(node_weight),
        row(dest_device),
        row(dest_cell),
        row(box_owner),
        row(box_slot),
    )
    arrived = exchange(packed, SENT, 1)
    load = scatter_rows(arrived, group, size_xy, size_z)
    load = load.reshape(3, size_x, size_y, size_z)
    adjoint = solve_sweeps(load, stiffness, anchor, coupling)
    partial = gather_rows(arrived, group, adjoint.reshape(3, size_xy, size_z))
    partial = exchange(partial.reshape(devices, 1, 3 * BOX_DEV), 1, 2)
    box_gradient = jnp.sum(partial, axis=(0, 1)).reshape(3, BOX_DEV)
    return (adjoint, box_gradient)


def solution(mesh):
    placed = (
        P(None, ("gx", "gy")),
        P(("gx", "gy")),
        P(("gx", "gy"), None),
        P(("gx", "gy")),
        P(("gx", "gy"), None),
        P(("gx", "gy")),
        P("gx", "gy", None),
        P(None, "gx", "gy", None),
        P(None, "gx", "gy", None),
    )
    return jax.shard_map(
        body,
        mesh=mesh,
        in_specs=placed,
        out_specs=(P(None, "gx", "gy", None), P(None, ("gx", "gy"))),
        check_vma=False,
    )
```

```python
import functools

import jax
import jax.numpy as jnp
from jax import lax
from jax.experimental import pallas as pl
from jax.experimental.pallas import tpu as pltpu
from jax.sharding import PartitionSpec as P

BOX_DEV = 64
SWEEPS = 4
SENT = 6
NT = (((1,), (1,)), ((), ()))
F32 = jnp.float32
BF16 = jnp.bfloat16
MESH = pl.DeviceIdType.MESH


def two_terms(x):
    hi = x.astype(BF16).astype(F32)
    return hi, x - hi


def matches(count, row):
    return lax.broadcasted_iota(jnp.int32, (count, row.shape[1]), 0) == row


def one_hot(mask):
    return jnp.where(mask, 1.0, 0.0).astype(BF16)


def scaled(mask, row):
    return jnp.where(mask, row, 0.0).astype(BF16)


def dot_nt(a, b):
    return lax.dot_general(a, b, NT, preferred_element_type=F32)


def pack_kernel(step, sens, weight, device, cell, owner, slot, out, tri, seen):
    targets, fields, capacity = out.shape
    rows = sens.shape[1]
    out[...] = jnp.zeros_like(out)
    seen[...] = jnp.zeros_like(seen)
    tri[...] = one_hot(
        lax.broadcasted_iota(jnp.int32, (step, step), 0)
        < lax.broadcasted_iota(jnp.int32, (step, step), 1)
    )

    def block(index, carry):
        span = pl.ds(pl.multiple_of(index * step, step), step)
        target = device[:, span]
        chosen = matches(targets, target)
        before = jnp.dot(one_hot(chosen), tri[...], preferred_element_type=F32) + seen[:, :1]
        rank = jnp.sum(jnp.where(chosen, before, 0.0), axis=0, keepdims=True).astype(jnp.int32)
        seen[...] = seen[...] + jnp.sum(jnp.where(chosen, 1.0, 0.0), axis=1, keepdims=True)
        place = one_hot(matches(capacity, rank))
        payload = jnp.concatenate(
            [
                sens[:, span],
                cell[:, span].astype(F32),
                weight[:, span],
                (owner[:, span] * BOX_DEV + slot[:, span]).astype(F32),
                jnp.zeros((fields - SENT, step), F32),
            ],
            axis=0,
        )
        wide = (targets, fields, step)
        to = lax.broadcasted_iota(jnp.int32, wide, 0) == target[None]
        terms = [
            jnp.where(to, term[None], 0.0).reshape(targets * fields, step).astype(BF16)
            for term in two_terms(payload)
        ]
        product = dot_nt(jnp.concatenate(terms, axis=0), place)
        product = product[: targets * fields] + product[targets * fields :]
        out[...] = out[...] + product.reshape(targets, fields, capacity)
        return carry

    lax.fori_loop(0, rows // step, block, 0)


def pack_rows(devices, capacity, sens, weight, device, cell, owner, slot):
    step = min(2048, sens.shape[1])
    return pl.pallas_call(
        functools.partial(pack_kernel, step),
        out_shape=jax.ShapeDtypeStruct((devices, 8, capacity), F32),
        in_specs=[pl.BlockSpec(memory_space=pltpu.VMEM)] * 6,
        out_specs=pl.BlockSpec(memory_space=pltpu.VMEM),
        scratch_shapes=[pltpu.VMEM((step, step), BF16), pltpu.VMEM((devices, 128), F32)],
        name="pack_rows",
    )(sens, weight, device, cell, owner, slot)


def joined(ref):
    return jnp.concatenate([ref[i, :SENT] for i in range(ref.shape[0])], axis=1)


def scatter_kernel(arrived, load, total):
    parts, size_xy, size_z = load.shape

    @pl.when(pl.program_id(0) == 0)
    def _():
        total[...] = jnp.zeros_like(total)

    block = joined(arrived)
    cell = block[3:4].astype(jnp.int32)
    at_z = matches(size_z, cell % size_z)
    at_xy = one_hot(matches(size_xy, cell // size_z))
    pairs = [two_terms(block[k : k + 1]) for k in range(parts)]
    terms = [scaled(at_z, hi) for hi, lo in pairs] + [scaled(at_z, lo) for hi, lo in pairs]
    product = dot_nt(jnp.concatenate(terms, axis=0), at_xy)
    half = parts * size_z
    total[...] = total[...] + product[:half] + product[half:]

    @pl.when(pl.program_id(0) == pl.num_programs(0) - 1)
    def _():
        for k in range(parts):
            load[k] = total[k * size_z : (k + 1) * size_z].T


def scatter_rows(arrived, group, size_xy, size_z):
    devices, fields, capacity = arrived.shape
    return pl.pallas_call(
        scatter_kernel,
        grid=(devices // group,),
        out_shape=jax.ShapeDtypeStruct((3, size_xy, size_z), F32),
        in_specs=[pl.BlockSpec((group, fields, capacity), lambda i: (i, 0, 0))],
        out_specs=pl.BlockSpec((3, size_xy, size_z), lambda i: (0, 0, 0)),
        scratch_shapes=[pltpu.VMEM((3 * size_z, size_xy), F32)],
        name="scatter_rows",
    )(arrived)


def gather_kernel(arrived, field, boxes, terms):
    parts, size_xy, size_z = field.shape
    devices = boxes.shape[0]

    @pl.when(pl.program_id(0) == 0)
    def _():
        boxes[...] = jnp.zeros_like(boxes)
        for k in range(parts):
            hi, lo = two_terms(field[k].T)
            terms[k * size_z : (k + 1) * size_z] = hi.astype(BF16)
            terms[(parts + k) * size_z : (parts + k + 1) * size_z] = lo.astype(BF16)

    block = joined(arrived)
    cell = block[3:4].astype(jnp.int32)
    at_z = matches(size_z, cell % size_z)
    at_xy = one_hot(matches(size_xy, cell // size_z))
    columns = jnp.dot(terms[...], at_xy, preferred_element_type=F32)
    box = block[5:6].astype(jnp.int32)
    at_owner = one_hot(matches(devices, box // BOX_DEV))
    at_slot = matches(BOX_DEV, box % BOX_DEV)
    for k in range(parts):
        column = columns[k * size_z : (k + 1) * size_z]
        column = column + columns[(parts + k) * size_z : (parts + k + 1) * size_z]
        value = jnp.sum(jnp.where(at_z, column, 0.0), axis=0, keepdims=True) * block[4:5]
        hi, lo = two_terms(value)
        part = dot_nt(at_owner, scaled(at_slot, hi)) + dot_nt(at_owner, scaled(at_slot, lo))
        boxes[:, k * BOX_DEV : (k + 1) * BOX_DEV] += part


def gather_rows(arrived, group, field):
    devices, fields, capacity = arrived.shape
    parts, size_xy, size_z = field.shape
    return pl.pallas_call(
        gather_kernel,
        grid=(devices // group,),
        out_shape=jax.ShapeDtypeStruct((devices, 3 * BOX_DEV), F32),
        in_specs=[
            pl.BlockSpec((group, fields, capacity), lambda i: (i, 0, 0)),
            pl.BlockSpec(memory_space=pltpu.VMEM),
        ],
        out_specs=pl.BlockSpec((devices, 3 * BOX_DEV), lambda i: (0, 0)),
        scratch_shapes=[pltpu.VMEM((2 * parts * size_z, size_xy), BF16)],
        name="gather_rows",
    )(arrived, field)


def sweep_kernel(load, stiff, anchor, coupling, adjoint, weighted, rest, inverse, edge, halo, x_send, x_recv, y_send, y_recv):
    parts, size_x, size_y, size_z = load.shape
    exchanges = weighted.shape[0]
    gx, gy = lax.axis_index("gx"), lax.axis_index("gy")
    last_x, last_y = lax.axis_size("gx") - 1, lax.axis_size("gy") - 1
    sides = (("gx", gx, -1, gx > 0), ("gx", gx, 1, gx < last_x), ("gy", gy, -1, gy > 0), ("gy", gy, 1, gy < last_y))
    y_at = lax.broadcasted_iota(jnp.int32, (size_y, size_z), 0)
    z_at = lax.broadcasted_iota(jnp.int32, (size_y, size_z), 1)

    for index in range(exchanges):
        for k in range(parts):
            weighted[index, k, 0] = jnp.zeros((size_y, size_z), F32)
            weighted[index, k, size_x + 1] = jnp.zeros((size_y, size_z), F32)
    halo[...] = jnp.zeros_like(halo)

    barrier = pltpu.get_barrier_semaphore()
    known = 0
    for axis, place, move, present in sides:
        known = known + present.astype(jnp.int32)

        @pl.when(present)
        def _():
            pl.semaphore_signal(barrier, inc=1, device_id={axis: place + move}, device_id_type=MESH)

    pl.semaphore_wait(barrier, known)

    def copies(index):
        made = []
        for side, (axis, place, move, present) in enumerate(sides):
            there = 1 - side % 2
            if axis == "gx":
                pair = (weighted.at[index, :, 1 if move < 0 else size_x], weighted.at[index, :, size_x + 1 if move < 0 else 0])
                sems = (x_send, x_recv)
            else:
                pair = (edge.at[index, side % 2], halo.at[index, there])
                sems = (y_send, y_recv)
            made.append((present, pltpu.make_async_remote_copy(
                src_ref=pair[0],
                dst_ref=pair[1],
                send_sem=sems[0].at[index, side % 2],
                recv_sem=sems[1].at[index, there],
                device_id={axis: place + move},
                device_id_type=MESH,
            )))
        return made

    def arrivals(index):
        made = []
        for side, (axis, place, move, present) in enumerate(sides):
            if axis == "gx":
                pair = (weighted.at[index, :, 1 if move < 0 else size_x], weighted.at[index, :, 0 if move < 0 else size_x + 1])
                sems = (x_send, x_recv)
            else:
                pair = (edge.at[index, side % 2], halo.at[index, side % 2])
                sems = (y_send, y_recv)
            made.append((present, pltpu.make_async_remote_copy(
                src_ref=pair[0],
                dst_ref=pair[1],
                send_sem=sems[0].at[index, side % 2],
                recv_sem=sems[1].at[index, side % 2],
                device_id={axis: place + move},
                device_id_type=MESH,
            )))
        return made

    def publish(index, x, k, value):
        adjoint[k, x] = value
        if index < exchanges:
            product = stiff[x] * value
            weighted[index, k, x + 1] = product
            edge[index, 0, k, pl.ds(x, 1), :] = product[0:1]
            edge[index, 1, k, pl.ds(x, 1), :] = product[size_y - 1 : size_y]

    def first(x, carry):
        for k in range(parts):
            inverse[k, x] = 1.0 / (6.0 * stiff[x] + anchor[k, x] + coupling[4 * k, x])
            publish(0, x, k, load[k, x] * inverse[k, x])
        return carry

    lax.fori_loop(0, size_x, first, 0)
    for index in range(exchanges):
        for present, copy in copies(index):

            @pl.when(present)
            def _():
                copy.start()

        def near(x, carry):
            fields = [adjoint[k, x] for k in range(parts)]
            for k in range(parts):
                product = weighted[index, k, x + 1]
                value = load[k, x] - 6.0 * product - anchor[k, x] * fields[k]
                for j in range(parts):
                    value = value - coupling[3 * j + k, x] * fields[j]
                value = value + jnp.where(z_at == 0, 0.0, pltpu.roll(product, 1, 1))
                value = value + jnp.where(z_at == size_z - 1, 0.0, pltpu.roll(product, size_z - 1, 1))
                value = value + jnp.where(y_at == 0, 0.0, pltpu.roll(product, 1, 0))
                value = value + jnp.where(y_at == size_y - 1, 0.0, pltpu.roll(product, size_y - 1, 0))
                rest[k, x] = value
            return carry

        lax.fori_loop(0, size_x, near, 0)
        for present, copy in arrivals(index):

            @pl.when(present)
            def _():
                copy.wait_recv()

        def far(x, carry):
            for k in range(parts):
                value = rest[k, x] + weighted[index, k, x] + weighted[index, k, x + 2]
                value = value + jnp.where(y_at == 0, halo[index, 0, k, pl.ds(x, 1), :], 0.0)
                value = value + jnp.where(y_at == size_y - 1, halo[index, 1, k, pl.ds(x, 1), :], 0.0)
                publish(index + 1, x, k, adjoint[k, x] + value * inverse[k, x])
            return carry

        lax.fori_loop(0, size_x, far, 0)
    for index in range(exchanges):
        for present, copy in copies(index):

            @pl.when(present)
            def _():
                copy.wait_send()


def solve_sweeps(load, stiffness, anchor, coupling):
    parts, size_x, size_y, size_z = load.shape
    exchanges = SWEEPS - 1
    return pl.pallas_call(
        sweep_kernel,
        out_shape=jax.ShapeDtypeStruct(load.shape, F32),
        in_specs=[pl.BlockSpec(memory_space=pltpu.VMEM)] * 4,
        out_specs=pl.BlockSpec(memory_space=pltpu.VMEM),
        scratch_shapes=[
            pltpu.VMEM((exchanges, parts, size_x + 2, size_y, size_z), F32),
            pltpu.VMEM(load.shape, F32),
            pltpu.VMEM(load.shape, F32),
            pltpu.VMEM((exchanges, 2, parts, size_x, size_z), F32),
            pltpu.VMEM((exchanges, 2, parts, size_x, size_z), F32),
        ]
        + [pltpu.SemaphoreType.DMA((exchanges, 2))] * 4,
        compiler_params=pltpu.CompilerParams(collective_id=0, has_side_effects=True),
        name="sweeps",
    )(load, stiffness, anchor, coupling)


def exchange_kernel(live, send, recv, send_sem, recv_sem, own_sem):
    count = send.shape[0]
    width = lax.axis_size("gy")
    me = lax.axis_index("gx") * width + lax.axis_index("gy")
    barrier = pltpu.get_barrier_semaphore()

    def device(index):
        return (index // width, index % width)

    def greet(step, carry):
        pl.semaphore_signal(barrier, inc=1, device_id=device((me + step) % count), device_id_type=MESH)
        return carry

    lax.fori_loop(1, count, greet, 0)
    pl.semaphore_wait(barrier, count - 1)

    def copy(step, source, landing):
        peer = (me + step) % count
        return pltpu.make_async_remote_copy(
            src_ref=send.at[source, pl.ds(0, live)],
            dst_ref=recv.at[landing, pl.ds(0, live)],
            send_sem=send_sem.at[step],
            recv_sem=recv_sem.at[step],
            device_id=device(peer),
            device_id_type=MESH,
        )

    def start(step, carry):
        copy(step, (me + step) % count, me).start()
        return carry

    lax.fori_loop(1, count, start, 0)
    own = pltpu.make_async_copy(send.at[me, pl.ds(0, live)], recv.at[me, pl.ds(0, live)], own_sem)
    own.start()

    def finish(step, carry):
        copy(step, (me + step) % count, (me + count - step) % count).wait_recv()
        copy(step, (me + step) % count, me).wait_send()
        return carry

    lax.fori_loop(1, count, finish, 0)
    own.wait()


def exchange(blocks, live, number):
    count = blocks.shape[0]
    return pl.pallas_call(
        functools.partial(exchange_kernel, live),
        out_shape=jax.ShapeDtypeStruct(blocks.shape, F32),
        in_specs=[pl.BlockSpec(memory_space=pltpu.VMEM)],
        out_specs=pl.BlockSpec(memory_space=pltpu.VMEM),
        scratch_shapes=[pltpu.SemaphoreType.DMA((count,))] * 2 + [pltpu.SemaphoreType.DMA],
        compiler_params=pltpu.CompilerParams(collective_id=number, has_side_effects=True),
        name="exchange_" + str(number),
    )(blocks)


def body(
    sensitivity,
    node_weight,
    dest_device,
    dest_cell,
    box_owner,
    box_slot,
    stiffness,
    anchor,
    coupling,
):
    devices = lax.axis_size("gx") * lax.axis_size("gy")
    row_count = sensitivity.shape[1]
    capacity = 2 * row_count // devices
    size_x, size_y, size_z = stiffness.shape
    size_xy = size_x * size_y
    assert size_xy * size_z <= 2**17 and devices * BOX_DEV <= 2**17
    group = max(1, min(devices, 2048 // capacity))

    def row(values):
        return values.reshape(1, row_count)

    packed = pack_rows(
        devices,
        capacity,
        sensitivity,
        row(node_weight),
        row(dest_device),
        row(dest_cell),
        row(box_owner),
        row(box_slot),
    )
    arrived = exchange(packed, SENT, 1)
    load = scatter_rows(arrived, group, size_xy, size_z)
    load = load.reshape(3, size_x, size_y, size_z)
    adjoint = solve_sweeps(load, stiffness, anchor, coupling)
    partial = gather_rows(arrived, group, adjoint.reshape(3, size_xy, size_z))
    partial = exchange(partial.reshape(devices, 1, 3 * BOX_DEV), 1, 2)
    box_gradient = jnp.sum(partial, axis=(0, 1)).reshape(3, BOX_DEV)
    return (adjoint, box_gradient)


def solution(mesh):
    placed = (
        P(None, ("gx", "gy")),
        P(("gx", "gy")),
        P(("gx", "gy"), None),
        P(("gx", "gy")),
        P(("gx", "gy"), None),
        P(("gx", "gy")),
        P("gx", "gy", None),
        P(None, "gx", "gy", None),
        P(None, "gx", "gy", None),
    )
    return jax.shard_map(
        body,
        mesh=mesh,
        in_specs=placed,
        out_specs=(P(None, "gx", "gy", None), P(None, ("gx", "gy"))),
        check_vma=False,
    )
```
